256 devices in a mesh: row: 32 (over y, x, core), col: 8 (over z).
Axes of the slice: x: 4, y: 4, z: 8, core: 2. Of those that a mesh axis runs over, the one named last changes fastest.
Arguments:
- panel: float32 [24576, 256], P('row', 'col'), may hold values from -6 to 6
- trailing: float32 [24576, 12032], P('row', 'col'), may hold values from -6 to 6
Outputs:
- projections: float32 [12032, 256], P('col')
- remainder: float32 [24576, 12032], P('row', 'col')
The draws below stay inside these ranges and needn't reach their ends.
All inputs are finite; a program needn't handle non-finite values.
Results may differ from the reference program's by a relative error of at most 0.000075.
Values sent between devices are 32-bit elements; how exact they have to be, the bound alone decides.
A program may use at most 64 MiB of HBM per device.

```python
import jax
import jax.numpy as jnp
from jax import lax

B = 256
TRAIL = 12032
ROWS = 24576


def levels(own_key, dims, split, smallest, high):
    def one(axis_at, blocks):
        steps = jax.random.uniform(jax.random.fold_in(jax.random.fold_in(own_key, 6), axis_at), (blocks,), jnp.float32, smallest / len(split), high / len(split))
        return jnp.repeat(jnp.exp(steps), dims[axis_at] // blocks).reshape((-1,) + (1,) * (len(dims) - axis_at - 1))

    loudness = one(*split[0])
    for cut in split[1:]:
        loudness = loudness * one(*cut)
    return loudness


def gaussian(rng, dims, deviation, limit, cuts=(), kind=jnp.bfloat16):
    array = deviation * jax.random.normal(rng, dims, jnp.float32)
    if cuts:
        array = array * levels(rng, dims, cuts, -0.22, 0.18)
    return jnp.clip(array, -limit, limit).astype(kind)


def setup_inputs(seed: int = 0) -> dict:
    keys = jax.random.split(jax.random.key(seed), 3)
    return {
        "panel": gaussian(keys[0], (ROWS, B), 1.0, 6.0, ((0, 32), (1, 8)), jnp.float32),
        "trailing": gaussian(keys[1], (ROWS, TRAIL), 1.0, 6.0, ((0, 32), (1, 8)), jnp.float32),
    }


def reference(panel, trailing):
    highest = lax.Precision.HIGHEST
    panel_gram = jnp.dot(panel.T.astype(jnp.float32), panel.astype(jnp.float32), precision=highest, preferred_element_type=jnp.float32)
    lower_factor = jnp.linalg.cholesky(panel_gram)
    orthonormal = jax.scipy.linalg.solve_triangular(lower_factor, panel.T, lower=True).T
    cross_terms = jnp.dot(trailing.T.astype(jnp.float32), panel.astype(jnp.float32), precision=highest, preferred_element_type=jnp.float32)
    projections = jax.scipy.linalg.solve_triangular(lower_factor, cross_terms.T, lower=True).T
    remainder = trailing - jnp.dot(orthonormal.astype(jnp.float32), projections.T.astype(jnp.float32), precision=highest, preferred_element_type=jnp.float32)
    return (projections, remainder)
```

```python
import jax
import jax.numpy as jnp
from jax import lax
from jax.experimental import pallas as pl
from jax.experimental.pallas import tpu as pltpu
from jax.sharding import PartitionSpec as P

F32 = jnp.float32
BF16 = jnp.bfloat16
MESH = pl.DeviceIdType.MESH
STEP = 16


def nt(left, right):
    return lax.dot_general(left, right, (((1,), (1,)), ((), ())), preferred_element_type=F32)


def nn(left, right):
    return lax.dot_general(left, right, (((1,), (0,)), ((), ())), preferred_element_type=F32)


def split2(x):
    high = x.astype(BF16)
    return high, (x - high.astype(F32)).astype(BF16)


def split3(x):
    high = x.astype(BF16).astype(F32)
    rest = x - high
    middle = rest.astype(BF16).astype(F32)
    return high, middle, rest - middle


def eliminate(m_ref, at):
    size = m_ref.shape[0]
    base = pl.multiple_of(at * STEP, STEP)
    rows = m_ref[pl.ds(base, STEP), :]
    turned = pltpu.roll(rows, size - at * STEP, 1)
    lane = lax.broadcasted_iota(jnp.int32, (STEP, size), 1)
    line = lax.broadcasted_iota(jnp.int32, (STEP, size), 0)
    line_narrow = lax.broadcasted_iota(jnp.int32, (STEP, 128), 0)
    columns = [jnp.broadcast_to(turned[:, j : j + 1], (STEP, 128)) for j in range(STEP)]
    inside = (lane >= base) & (lane < base + STEP)
    rows = jnp.where(inside, jnp.where(lane - base == line, 1.0, 0.0), rows)
    parts = [rows[:, p : p + 128] for p in range(0, size, 128)]
    for j in range(STEP):
        scale = lax.rsqrt(columns[j][j : j + 1, :])
        lower = jnp.where(line_narrow > j, columns[j] * scale, 0.0)
        for k in range(j + 1, STEP):
            columns[k] = columns[k] - lower * (columns[k][j : j + 1, :] * scale)
        for p in range(len(parts)):
            scaled = parts[p][j : j + 1, :] * scale
            parts[p] = jnp.where(line_narrow == j, scaled, parts[p] - lower * scaled)
    rows = jnp.concatenate(parts, 1)
    m_ref[pl.ds(base, STEP), :] = rows
    high, middle, low = split3(rows)
    left = jnp.concatenate([high, high, middle, high, middle, low], 0).astype(BF16)
    right = jnp.concatenate([high, middle, high, low, middle, high], 0).astype(BF16)
    change = lax.dot_general(left, right, (((0,), (0,)), ((), ())), preferred_element_type=F32)
    line_all = lax.broadcasted_iota(jnp.int32, (size, size), 0)
    lane_all = lax.broadcasted_iota(jnp.int32, (size, size), 1)
    whole = m_ref[...]
    inside = (lane_all >= base) & (lane_all < base + STEP)
    m_ref[...] = jnp.where(line_all >= base + STEP, jnp.where(inside, 0.0, whole) - change, whole)


def reduce_kernel(
    a_ref, t_ref, full_ref, inv_ref, c_ref,
    t_mem, t_high, t_low, g_part, g_recv, g_own, g_full, c_part, c_pair, c_recv, c_own,
    t_sem, ag_send, ag_recv, grs_send, grs_recv, gag_send, gag_recv,
    pair_send, pair_recv, crs_send, crs_recv, cag_send, cag_recv, last_send, last_recv,
):
    me = lax.axis_index("row")
    z = lax.axis_index("col")
    n_row = lax.axis_size("row")
    n_col = lax.axis_size("col")
    chip, core = me // 2, lax.rem(me, 2)
    n_chip = n_row // 2
    wide = a_ref.shape[0]
    n_b = full_ref.shape[0]
    n_t = t_ref.shape[0]
    half = c_part.shape[0] // 2
    block = half // n_chip
    own = n_b // n_row
    right, left = lax.rem(z + 1, n_col), lax.rem(z + n_col - 1, n_col)

    tile = half // 2
    loads = []
    for i in range(4):
        size = min(tile, n_t - i * tile)
        loads.append(pltpu.make_async_copy(t_ref.at[pl.ds(i * tile, size), :], t_mem.at[pl.ds(i * tile, size), :], t_sem.at[i]))
        loads[-1].start()

    barrier = pltpu.get_barrier_semaphore()
    for there in (left, right):
        pl.semaphore_signal(barrier, inc=1, device_id=(me, there), device_id_type=MESH)

    def greet(i, carry):
        pl.semaphore_signal(barrier, inc=1, device_id=(lax.rem(me + i, n_row), z), device_id_type=MESH)
        return carry

    lax.fori_loop(1, n_row, greet, 0)
    pl.semaphore_wait(barrier, n_row + 1)

    piece = 8
    n_piece = wide // piece

    def hop(way, step, q):
        owner = lax.rem(z - step + n_col, n_col) if way == 0 else lax.rem(z + step, n_col)
        place = pl.ds(pl.multiple_of(owner * wide + q * piece, piece), piece)
        source = a_ref.at[pl.ds(q * piece, piece), :] if step == 0 else full_ref.at[place, :]
        return pltpu.make_async_remote_copy(
            src_ref=source,
            dst_ref=full_ref.at[place, :],
            send_sem=ag_send.at[way, step, q],
            recv_sem=ag_recv.at[way, step, q],
            device_id=(me, right if way == 0 else left),
            device_id_type=MESH,
        )

    def taken(way, step):
        if step < n_col // 2 - 1:
            return range(n_piece)
        return range(n_piece // 2) if way == 0 else range(n_piece // 2, n_piece)

    hops = []
    for q in range(n_piece):
        for way in range(2):
            hops.append(hop(way, 0, q))
            hops[-1].start()
    full_ref[pl.ds(pl.multiple_of(z * wide, wide), wide), :] = a_ref[...]
    t_high[n_t:, :] = jnp.zeros((2 * half - n_t, t_high.shape[1]), BF16)
    t_low[n_t:, :] = jnp.zeros((2 * half - n_t, t_high.shape[1]), BF16)

    for step in range(n_col // 2):
        for q in range(n_piece):
            for way in range(2):
                if q in taken(way, step):
                    hop(way, step, q).wait_recv()
                    if step + 1 < n_col // 2 and q in taken(way, step + 1):
                        hops.append(hop(way, step + 1, q))
                        hops[-1].start()
        if step < 2:
            for i in (2 * step, 2 * step + 1):
                loads[i].wait()
                size = min(tile, n_t - i * tile)

                @pl.loop(0, size // 32)
                def _(k):
                    there = pl.ds(pl.multiple_of(i * tile + k * 32, 32), 32)
                    high, low = split2(t_mem[there, :])
                    t_high[there, :] = high
                    t_low[there, :] = low

    for copy in hops:
        copy.wait_send()

    full = full_ref[...]
    g_part[...] = lax.dot_general(full, full, (((1,), (1,)), ((), ())), precision=lax.Precision.HIGHEST, preferred_element_type=F32)

    def g_send(i, carry):
        there = lax.rem(me + i, n_row)
        pltpu.make_async_remote_copy(
            src_ref=g_part.at[pl.ds(pl.multiple_of(there * own, own), own), :],
            dst_ref=g_recv.at[me],
            send_sem=grs_send,
            recv_sem=grs_recv,
            device_id=(there, z),
            device_id_type=MESH,
        ).start()
        return carry

    lax.fori_loop(1, n_row, g_send, 0)
    g_recv[me] = g_part[pl.ds(pl.multiple_of(me * own, own), own), :]

    a_high, a_low = split2(full)

    def cross(start, size):
        for k in range(0, size, size // 4):
            there = pl.ds(pl.multiple_of(start + k, 16), size // 4)
            high, low = t_high[there, :], t_low[there, :]
            c_part[there, :] = nt(high, a_high) + (nt(high, a_low) + nt(low, a_high))

    cross((1 - core) * half, half)
    pair = pltpu.make_async_remote_copy(
        src_ref=c_part.at[pl.ds(pl.multiple_of((1 - core) * half, half), half), :],
        dst_ref=c_pair,
        send_sem=pair_send,
        recv_sem=pair_recv,
        device_id=(me + 1 - 2 * core, z),
        device_id_type=MESH,
    )
    pair.start()

    everyone = pl.ds(0, n_row - 1)
    pltpu.make_async_copy(g_recv.at[everyone], g_recv.at[everyone], grs_recv).wait()
    g_own[...] = jnp.sum(g_recv[...], axis=0)

    def g_spread(i, carry):
        pltpu.make_async_remote_copy(
            src_ref=g_own,
            dst_ref=g_full.at[pl.ds(pl.multiple_of(me * own, own), own), :],
            send_sem=gag_send,
            recv_sem=gag_recv,
            device_id=(lax.rem(me + i, n_row), z),
            device_id_type=MESH,
        ).start()
        return carry

    lax.fori_loop(1, n_row, g_spread, 0)
    g_full[pl.ds(pl.multiple_of(me * own, own), own), :] = g_own[...]

    cross(core * half, half)
    pair.wait()
    mine = pl.multiple_of(core * half, half)

    @pl.loop(0, n_chip)
    def _(k):
        there = pl.ds(pl.multiple_of(k * block, block), block)
        c_pair[there, :] = c_pair[there, :] + c_part[pl.ds(pl.multiple_of(mine + k * block, block), block), :]

    def c_send(i, carry):
        there = lax.rem(chip + i, n_chip)
        pltpu.make_async_remote_copy(
            src_ref=c_pair.at[pl.ds(pl.multiple_of(there * block, block), block), :],
            dst_ref=c_recv.at[chip],
            send_sem=crs_send,
            recv_sem=crs_recv,
            device_id=(there * 2 + core, z),
            device_id_type=MESH,
        ).start()
        return carry

    lax.fori_loop(1, n_chip, c_send, 0)
    c_recv[chip] = c_pair[pl.ds(pl.multiple_of(chip * block, block), block), :]

    rest = pl.ds(0, (n_row - 1) * own)
    pltpu.make_async_copy(g_full.at[rest, :], g_full.at[rest, :], gag_recv).wait()

    def some(at, carry):
        eliminate(g_full, at)
        return carry

    lax.fori_loop(0, 10, some, 0)

    others = pl.ds(0, n_chip - 1)
    pltpu.make_async_copy(c_recv.at[others], c_recv.at[others], crs_recv).wait()
    c_own[...] = jnp.sum(c_recv[...], axis=0)
    here = pl.ds(pl.multiple_of(mine + chip * block, block), block)

    def c_spread(i, carry):
        pltpu.make_async_remote_copy(
            src_ref=c_own,
            dst_ref=c_ref.at[here, :],
            send_sem=cag_send,
            recv_sem=cag_recv,
            device_id=(lax.rem(chip + i, n_chip) * 2 + core, z),
            device_id_type=MESH,
        ).start()
        return carry

    lax.fori_loop(1, n_chip, c_spread, 0)
    c_ref[here, :] = c_own[...]
    lax.fori_loop(10, n_b // STEP, some, 0)
    line = lax.broadcasted_iota(jnp.int32, (n_b, n_b), 0)
    lane = lax.broadcasted_iota(jnp.int32, (n_b, n_b), 1)
    inv_ref[...] = jnp.where(line >= lane, g_full[...], 0.0)

    fetched = pl.ds(0, (n_chip - 1) * block)
    pltpu.make_async_copy(c_ref.at[fetched, :], c_ref.at[fetched, :], cag_recv).wait()
    held = pl.ds(mine, half)
    last = pltpu.make_async_remote_copy(
        src_ref=c_ref.at[held, :],
        dst_ref=c_ref.at[held, :],
        send_sem=last_send,
        recv_sem=last_recv,
        device_id=(me + 1 - 2 * core, z),
        device_id_type=MESH,
    )
    last.start()
    pltpu.make_async_copy(g_recv.at[everyone], g_recv.at[everyone], grs_send).wait()
    pltpu.make_async_copy(g_full.at[rest, :], g_full.at[rest, :], gag_send).wait()
    pltpu.make_async_copy(c_recv.at[others], c_recv.at[others], crs_send).wait()
    pltpu.make_async_copy(c_ref.at[fetched, :], c_ref.at[fetched, :], cag_send).wait()
    last.wait()


def reduce_call(a, t, n_row, n_col):
    wide, rows = a.shape
    n_b = wide * n_col
    n_t = t.shape[0]
    unit = n_row * 16
    padded = -(-n_t // unit) * unit
    half, n_chip = padded // 2, n_row // 2
    block = half // n_chip
    own = n_b // n_row
    vmem = pl.BlockSpec(memory_space=pltpu.VMEM)
    dma = pltpu.SemaphoreType.DMA
    return pl.pallas_call(
        reduce_kernel,
        out_shape=(
            jax.ShapeDtypeStruct((n_b, rows), F32),
            jax.ShapeDtypeStruct((n_b, n_b), F32),
            jax.ShapeDtypeStruct((padded, n_b), F32),
        ),
        in_specs=[vmem, pl.BlockSpec(memory_space=pl.ANY)],
        out_specs=(vmem, vmem, vmem),
        scratch_shapes=[
            pltpu.VMEM((n_t, rows), F32),
            pltpu.VMEM((padded, rows), BF16),
            pltpu.VMEM((padded, rows), BF16),
            pltpu.VMEM((n_b, n_b), F32),
            pltpu.VMEM((n_row, own, n_b), F32),
            pltpu.VMEM((own, n_b), F32),
            pltpu.VMEM((n_b, n_b), F32),
            pltpu.VMEM((padded, n_b), F32),
            pltpu.VMEM((half, n_b), F32),
            pltpu.VMEM((n_chip, block, n_b), F32),
            pltpu.VMEM((block, n_b), F32),
            dma((4,)),
            dma((2, n_col // 2, wide // 8)),
            dma((2, n_col // 2, wide // 8)),
        ] + [dma] * 12,
        compiler_params=pltpu.CompilerParams(collective_id=0, has_side_effects=True, vmem_limit_bytes=48 * 2**20),
    )(a, t)


def update_kernel(full_ref, inv_ref, c_ref, t_ref, p_ref, r_ref, q_high, q_low):
    high, low = split2(inv_ref[...])

    @pl.when(pl.program_id(0) == 0)
    def _():
        a_high, a_low = split2(full_ref[...])
        q = nn(high, a_high) + (nn(high, a_low) + nn(low, a_high))
        q_high[...], q_low[...] = split2(q)

    c_high, c_low = split2(c_ref[...])
    p = nt(c_high, high) + (nt(c_high, low) + nt(c_low, high))
    p_ref[...] = p
    p_high, p_low = split2(p)
    r_ref[...] = t_ref[...] - (nn(p_high, q_high[...]) + (nn(p_high, q_low[...]) + nn(p_low, q_high[...])))


def update_call(full, inverse, c, t, tiles=4):
    n_b, rows = full.shape
    n_t = t.shape[0]
    tile = n_t // tiles
    return pl.pallas_call(
        update_kernel,
        grid=(tiles,),
        out_shape=(jax.ShapeDtypeStruct((n_t, n_b), F32), jax.ShapeDtypeStruct((n_t, rows), F32)),
        in_specs=[
            pl.BlockSpec((n_b, rows), lambda i: (0, 0)),
            pl.BlockSpec((n_b, n_b), lambda i: (0, 0)),
            pl.BlockSpec((tile, n_b), lambda i: (i, 0)),
            pl.BlockSpec((tile, rows), lambda i: (i, 0)),
        ],
        out_specs=(pl.BlockSpec((tile, n_b), lambda i: (i, 0)), pl.BlockSpec((tile, rows), lambda i: (i, 0))),
        scratch_shapes=[pltpu.VMEM((n_b, rows), BF16), pltpu.VMEM((n_b, rows), BF16)],
        compiler_params=pltpu.CompilerParams(vmem_limit_bytes=40 * 2**20),
    )(full, inverse, c, t)


def solution(mesh):
    n_row, n_col = mesh.shape["row"], mesh.shape["col"]

    def per_device(panel, trailing):
        a, t = panel.T, trailing.T
        full, inverse, c = reduce_call(a, t, n_row, n_col)
        projections, remainder = update_call(full, inverse, c, t)
        return projections, remainder.T

    return jax.shard_map(
        per_device,
        mesh=mesh,
        in_specs=(P("row", "col"), P("row", "col")),
        out_specs=(P("col", None), P("row", "col")),
        check_vma=False,
    )
```

```python
import jax
import jax.numpy as jnp
from jax import lax
from jax.experimental import pallas as pl
from jax.experimental.pallas import tpu as pltpu
from jax.sharding import PartitionSpec as P

F32 = jnp.float32
BF16 = jnp.bfloat16
MESH = pl.DeviceIdType.MESH
STEP = 16
SIDE = 4
TILE = 256


def nt(left, right):
    return lax.dot_general(left, right, (((1,), (1,)), ((), ())), preferred_element_type=F32)


def nn(left, right):
    return lax.dot_general(left, right, (((1,), (0,)), ((), ())), preferred_element_type=F32)


def split2(x):
    high = x.astype(BF16)
    return high, (x - high.astype(F32)).astype(BF16)


def split3(x):
    high = x.astype(BF16).astype(F32)
    rest = x - high
    middle = rest.astype(BF16).astype(F32)
    return high, middle, rest - middle


def eliminate(m_ref, at):
    size = m_ref.shape[0]
    base = pl.multiple_of(at * STEP, STEP)
    rows = m_ref[pl.ds(base, STEP), :]
    turned = pltpu.roll(rows, size - at * STEP, 1)
    lane = lax.broadcasted_iota(jnp.int32, (STEP, size), 1)
    line = lax.broadcasted_iota(jnp.int32, (STEP, size), 0)
    line_narrow = lax.broadcasted_iota(jnp.int32, (STEP, 128), 0)
    columns = [jnp.broadcast_to(turned[:, j : j + 1], (STEP, 128)) for j in range(STEP)]
    inside = (lane >= base) & (lane < base + STEP)
    rows = jnp.where(inside, jnp.where(lane - base == line, 1.0, 0.0), rows)
    parts = [rows[:, p : p + 128] for p in range(0, size, 128)]
    for j in range(STEP):
        scale = lax.rsqrt(columns[j][j : j + 1, :])
        lower = jnp.where(line_narrow > j, columns[j] * scale, 0.0)
        for k in range(j + 1, STEP):
            columns[k] = columns[k] - lower * (columns[k][j : j + 1, :] * scale)
        for p in range(len(parts)):
            scaled = parts[p][j : j + 1, :] * scale
            parts[p] = jnp.where(line_narrow == j, scaled, parts[p] - lower * scaled)
    rows = jnp.concatenate(parts, 1)
    m_ref[pl.ds(base, STEP), :] = rows
    high, middle, low = split3(rows)
    left = jnp.concatenate([high, high, middle, high, middle, low], 0).astype(BF16)
    right = jnp.concatenate([high, middle, high, low, middle, high], 0).astype(BF16)
    change = lax.dot_general(left, right, (((0,), (0,)), ((), ())), preferred_element_type=F32)
    line_all = lax.broadcasted_iota(jnp.int32, (size, size), 0)
    lane_all = lax.broadcasted_iota(jnp.int32, (size, size), 1)
    whole = m_ref[...]
    inside = (lane_all >= base) & (lane_all < base + STEP)
    m_ref[...] = jnp.where(line_all >= base + STEP, jnp.where(inside, 0.0, whole) - change, whole)


def reduce_kernel(
    a_ref, t_ref, p_ref, qh_ref, ql_ref,
    full, t_mem, t_high, t_low, g_part, g_low, g_high, low_own, high_own, g_full, c_part, c_pair, c_recv, c_own, c_all, inv_high, inv_low,
    met, t_sem, a_sem, ag_send, ag_recv, low_send, low_recv, high_send, high_recv, lag_send, lag_recv, hag_send, hag_recv,
    pair_send, pair_recv, crs_send, crs_recv, cag_send, cag_recv, last_send, last_recv,
):
    me = lax.axis_index("row")
    z = lax.axis_index("col")
    n_row = lax.axis_size("row")
    n_col = lax.axis_size("col")
    chip, core = me // 2, lax.rem(me, 2)
    n_chip = n_row // 2
    y, x = chip // SIDE, lax.rem(chip, SIDE)
    wide = a_ref.shape[0]
    n_b = full.shape[0]
    n_t = t_ref.shape[0]
    half = c_part.shape[0] // 2
    block = half // n_chip
    low_rows = n_b // 2
    own = low_rows // n_chip
    right, left = lax.rem(z + 1, n_col), lax.rem(z + n_col - 1, n_col)
    partner = me + 1 - 2 * core

    def sit(row, column, on):
        return (row * SIDE + column) * 2 + on

    x_near = [sit(y, lax.rem(x + k, SIDE), core) for k in (1, SIDE - 1)]
    y_near = [sit(lax.rem(y + k, SIDE), x, core) for k in (1, SIDE - 1)]

    barrier = pltpu.get_barrier_semaphore()
    for there in (left, right):
        pl.semaphore_signal(barrier, inc=1, device_id=(me, there), device_id_type=MESH)
    for there in x_near + y_near + [partner]:
        pl.semaphore_signal(barrier, inc=1, device_id=(there, z), device_id_type=MESH)

    tile = half // 2
    loads = []
    for i in range(4):
        size = min(tile, n_t - i * tile)
        loads.append(pltpu.make_async_copy(t_ref.at[pl.ds(i * tile, size), :], t_mem.at[pl.ds(i * tile, size), :], t_sem.at[i]))
        loads[-1].start()
    own_panel = pltpu.make_async_copy(a_ref, full.at[pl.ds(pl.multiple_of(z * wide, wide), wide), :], a_sem)
    own_panel.start()
    pl.semaphore_wait(barrier, 7)

    def meet(stage):
        near = (x_near, y_near, y_near, [partner])[stage]
        for there in near:
            pl.semaphore_signal(met.at[stage], inc=1, device_id=(there, z), device_id_type=MESH)

    def met_all(stage):
        pl.semaphore_wait(met.at[stage], (2, 2, 2, 1)[stage])

    piece = 8
    n_piece = wide // piece

    def hop(way, step, q):
        owner = lax.rem(z - step + n_col, n_col) if way == 0 else lax.rem(z + step, n_col)
        place = pl.ds(pl.multiple_of(owner * wide + q * piece, piece), piece)
        source = a_ref.at[pl.ds(q * piece, piece), :] if step == 0 else full.at[place, :]
        return pltpu.make_async_remote_copy(
            src_ref=source,
            dst_ref=full.at[place, :],
            send_sem=ag_send.at[way, step, q],
            recv_sem=ag_recv.at[way, step, q],
            device_id=(me, right if way == 0 else left),
            device_id_type=MESH,
        )

    def taken(way, step):
        if step < n_col // 2 - 1:
            return range(n_piece)
        return range(n_piece // 2) if way == 0 else range(n_piece // 2, n_piece)

    hops = []
    for q in range(n_piece):
        for way in range(2):
            hops.append(hop(way, 0, q))
            hops[-1].start()
    meet(0)
    t_high[n_t:, :] = jnp.zeros((2 * half - n_t, t_high.shape[1]), BF16)
    t_low[n_t:, :] = jnp.zeros((2 * half - n_t, t_high.shape[1]), BF16)
    g_full[low_rows:, :low_rows] = jnp.zeros((n_b - low_rows, low_rows), F32)

    slot = 0
    slots = n_piece * (n_col // 2)
    share = 2 * half // slots
    for step in range(n_col // 2):
        for q in range(n_piece):
            first = slot * share
            if first % tile == 0:
                loads[first // tile].wait()
            count = min(share, n_t - first) // 32

            @pl.loop(0, count)
            def _(k):
                there = pl.ds(pl.multiple_of(first + k * 32, 32), 32)
                high, low = split2(t_mem[there, :])
                t_high[there, :] = high
                t_low[there, :] = low

            slot += 1
            for way in range(2):
                if q in taken(way, step):
                    hop(way, step, q).wait_recv()
                    if step + 1 < n_col // 2 and q in taken(way, step + 1):
                        hops.append(hop(way, step + 1, q))
                        hops[-1].start()
        met_all(step)
        if step < 3:
            meet(step + 1)

    own_panel.wait()
    a_full = full[...]
    g_part[...] = lax.dot_general(a_full, a_full, (((1,), (1,)), ((), ())), precision=lax.Precision.HIGHEST, preferred_element_type=F32)

    def low_at(k):
        return pl.ds(pl.multiple_of(k * own, own), own)

    def high_at(k):
        return pl.ds(pl.multiple_of(low_rows + k * own, own), own)

    upper = pl.ds(low_rows, n_b - low_rows)

    def low_copy(there):
        return pltpu.make_async_remote_copy(
            src_ref=g_part.at[low_at(there), :], dst_ref=g_low.at[me], send_sem=low_send, recv_sem=low_recv,
            device_id=(there * 2, z), device_id_type=MESH)

    def high_copy(there):
        return pltpu.make_async_remote_copy(
            src_ref=g_part.at[high_at(there), upper], dst_ref=g_high.at[me], send_sem=high_send, recv_sem=high_recv,
            device_id=(there * 2 + 1, z), device_id_type=MESH)

    def each_chip(start):
        def body(i, carry):
            start(lax.rem(chip + i, n_chip))
            return carry

        lax.fori_loop(1, n_chip, body, 0)

    each_chip(lambda there: low_copy(there).start())

    @pl.when(core == 1)
    def _():
        low_copy(chip).start()

    each_chip(lambda there: high_copy(there).start())

    @pl.when(core == 0)
    def _():
        high_copy(chip).start()
        g_low[me] = g_part[low_at(chip), :]

    @pl.when(core == 1)
    def _():
        g_high[me] = g_part[high_at(chip), low_rows:]

    a_high, a_low = split2(a_full)

    def cross(start, size):
        for k in range(0, size, size // 4):
            there = pl.ds(pl.multiple_of(start + k, 16), size // 4)
            high, low = t_high[there, :], t_low[there, :]
            c_part[there, :] = nt(high, a_high) + (nt(high, a_low) + nt(low, a_high))

    cross((1 - core) * half, half)
    pair = pltpu.make_async_remote_copy(
        src_ref=c_part.at[pl.ds(pl.multiple_of((1 - core) * half, half), half), :],
        dst_ref=c_pair,
        send_sem=pair_send,
        recv_sem=pair_recv,
        device_id=(partner, z),
        device_id_type=MESH,
    )
    pair.start()

    def await_all(ref, sem):
        pltpu.make_async_copy(ref, ref, sem).wait()

    def each_row(start):
        def body(i, carry):
            start(lax.rem(me + i, n_row))
            return carry

        lax.fori_loop(1, n_row, body, 0)

    @pl.when(core == 0)
    def _():
        await_all(g_low.at[pl.ds(0, n_row - 1)], low_recv)
        low_own[...] = jnp.sum(g_low[...], axis=0)
        each_row(lambda there: pltpu.make_async_remote_copy(
            src_ref=low_own, dst_ref=g_full.at[low_at(chip), :], send_sem=lag_send, recv_sem=lag_recv,
            device_id=(there, z), device_id_type=MESH).start())
        g_full[low_at(chip), :] = low_own[...]

    @pl.when(core == 1)
    def _():
        await_all(g_high.at[pl.ds(0, n_row - 1)], high_recv)
        high_own[...] = jnp.sum(g_high[...], axis=0)
        each_row(lambda there: pltpu.make_async_remote_copy(
            src_ref=high_own, dst_ref=g_full.at[high_at(chip), upper], send_sem=hag_send, recv_sem=hag_recv,
            device_id=(there, z), device_id_type=MESH).start())
        g_full[high_at(chip), low_rows:] = high_own[...]

    cross(core * half, half)
    pair.wait()
    mine = pl.multiple_of(core * half, half)

    @pl.loop(0, n_chip)
    def _(k):
        there = pl.ds(pl.multiple_of(k * block, block), block)
        c_pair[there, :] = c_pair[there, :] + c_part[pl.ds(pl.multiple_of(mine + k * block, block), block), :]

    each_chip(lambda there: pltpu.make_async_remote_copy(
        src_ref=c_pair.at[pl.ds(pl.multiple_of(there * block, block), block), :],
        dst_ref=c_recv.at[chip],
        send_sem=crs_send,
        recv_sem=crs_recv,
        device_id=(there * 2 + core, z),
        device_id_type=MESH,
    ).start())
    c_recv[chip] = c_pair[pl.ds(pl.multiple_of(chip * block, block), block), :]

    few = (n_chip - 1) * own

    @pl.when(core == 0)
    def _():
        await_all(g_full.at[pl.ds(0, few), :], lag_recv)
        await_all(g_full.at[pl.ds(low_rows, few + own), upper], hag_recv)

    @pl.when(core == 1)
    def _():
        await_all(g_full.at[pl.ds(0, few + own), :], lag_recv)
        await_all(g_full.at[pl.ds(low_rows, few), upper], hag_recv)

    def some(at, carry):
        eliminate(g_full, at)
        return carry

    lax.fori_loop(0, 10, some, 0)

    others = pl.ds(0, n_chip - 1)
    await_all(c_recv.at[others], crs_recv)
    c_own[...] = jnp.sum(c_recv[...], axis=0)
    here = pl.ds(pl.multiple_of(chip * block, block), block)
    each_chip(lambda there: pltpu.make_async_remote_copy(
        src_ref=c_own,
        dst_ref=c_all.at[here, :],
        send_sem=cag_send,
        recv_sem=cag_recv,
        device_id=(there * 2 + core, z),
        device_id_type=MESH,
    ).start())
    c_all[here, :] = c_own[...]
    lax.fori_loop(10, n_b // STEP, some, 0)

    line = lax.broadcasted_iota(jnp.int32, (n_b, n_b), 0)
    lane = lax.broadcasted_iota(jnp.int32, (n_b, n_b), 1)
    high, low = split2(jnp.where(line >= lane, g_full[...], 0.0))
    inv_high[...] = high
    inv_low[...] = low
    a_high, a_low = split2(full[...])
    q = nn(high, a_high) + (nn(high, a_low) + nn(low, a_high))
    qh_ref[...], ql_ref[...] = split2(q)

    fetched = pl.ds(0, (n_chip - 1) * block)
    await_all(c_all.at[fetched, :], cag_recv)
    quarter = half // 4
    lasts = []
    for k in range(4):
        there = pl.ds(k * quarter, quarter)
        c_high, c_low = split2(c_all[there, :])
        held = pl.ds(pl.multiple_of(mine + k * quarter, quarter), quarter)
        p_ref[held, :] = nt(c_high, inv_high[...]) + (nt(c_high, inv_low[...]) + nt(c_low, inv_high[...]))
        lasts.append(pltpu.make_async_remote_copy(
            src_ref=p_ref.at[held, :],
            dst_ref=p_ref.at[held, :],
            send_sem=last_send.at[k],
            recv_sem=last_recv.at[k],
            device_id=(partner, z),
            device_id_type=MESH,
        ))
        lasts[-1].start()

    for copy in hops:
        copy.wait_send()

    @pl.when(core == 0)
    def _():
        await_all(g_low.at[others], low_send)
        await_all(g_high.at[pl.ds(0, n_chip)], high_send)
        await_all(g_low.at[pl.ds(0, n_row - 1)], lag_send)

    @pl.when(core == 1)
    def _():
        await_all(g_low.at[pl.ds(0, n_chip)], low_send)
        await_all(g_high.at[others], high_send)
        await_all(g_high.at[pl.ds(0, n_row - 1)], hag_send)

    await_all(c_recv.at[others], crs_send)
    await_all(c_all.at[fetched, :], cag_send)
    for copy in lasts:
        copy.wait()


def reduce_call(a, t, n_row, n_col):
    wide, rows = a.shape
    n_b = wide * n_col
    n_t = t.shape[0]
    unit = n_row * 16
    padded = -(-n_t // unit) * unit
    half, n_chip = padded // 2, n_row // 2
    block = half // n_chip
    own = n_b // n_row
    vmem = pl.BlockSpec(memory_space=pltpu.VMEM)
    dma = pltpu.SemaphoreType.DMA
    return pl.pallas_call(
        reduce_kernel,
        out_shape=(
            jax.ShapeDtypeStruct((padded, n_b), F32),
            jax.ShapeDtypeStruct((n_b, rows), BF16),
            jax.ShapeDtypeStruct((n_b, rows), BF16),
        ),
        in_specs=[pl.BlockSpec(memory_space=pl.ANY), pl.BlockSpec(memory_space=pl.ANY)],
        out_specs=(vmem, vmem, vmem),
        scratch_shapes=[
            pltpu.VMEM((n_b, rows), F32),
            pltpu.VMEM((n_t, rows), F32),
            pltpu.VMEM((padded, rows), BF16),
            pltpu.VMEM((padded, rows), BF16),
            pltpu.VMEM((n_b, n_b), F32),
            pltpu.VMEM((n_row, own, n_b), F32),
            pltpu.VMEM((n_row, own, n_b // 2), F32),
            pltpu.VMEM((own, n_b), F32),
            pltpu.VMEM((own, n_b // 2), F32),
            pltpu.VMEM((n_b, n_b), F32),
            pltpu.VMEM((padded, n_b), F32),
            pltpu.VMEM((half, n_b), F32),
            pltpu.VMEM((n_chip, block, n_b), F32),
            pltpu.VMEM((block, n_b), F32),
            pltpu.VMEM((half, n_b), F32),
            pltpu.VMEM((n_b, n_b), BF16),
            pltpu.VMEM((n_b, n_b), BF16),
            pltpu.SemaphoreType.REGULAR((4,)),
            dma((4,)),
            dma,
            dma((2, n_col // 2, wide // 8)),
            dma((2, n_col // 2, wide // 8)),
        ] + [dma] * 14 + [dma((4,))] * 2,
        compiler_params=pltpu.CompilerParams(collective_id=0, has_side_effects=True, vmem_limit_bytes=48 * 2**20),
    )(a, t)


def update_kernel(p_ref, qh_ref, ql_ref, t_ref, p_out, r_out, r_mem, p_sem, r_sem):
    n_t = t_ref.shape[0]
    first = pltpu.make_async_copy(p_ref.at[pl.ds(0, n_t), :], p_out, p_sem)
    first.start()
    q_high, q_low = qh_ref[...], ql_ref[...]
    copies = []
    for i, start in enumerate(range(0, n_t, TILE)):
        there = pl.ds(start, min(TILE, n_t - start))
        p_high, p_low = split2(p_ref[there, :])
        r_mem[there, :] = t_ref[there, :] - (nn(p_high, q_high) + (nn(p_high, q_low) + nn(p_low, q_high)))
        copies.append(pltpu.make_async_copy(r_mem.at[there, :], r_out.at[there, :], r_sem.at[i]))
        copies[-1].start()
    first.wait()
    for copy in copies:
        copy.wait()


def update_call(p, q_high, q_low, t):
    n_b, rows = q_high.shape
    n_t = t.shape[0]
    vmem = pl.BlockSpec(memory_space=pltpu.VMEM)
    hbm = pl.BlockSpec(memory_space=pltpu.HBM)
    return pl.pallas_call(
        update_kernel,
        out_shape=(jax.ShapeDtypeStruct((n_t, n_b), F32), jax.ShapeDtypeStruct((n_t, rows), F32)),
        in_specs=[vmem] * 4,
        out_specs=(hbm, hbm),
        scratch_shapes=[
            pltpu.VMEM((n_t, rows), F32),
            pltpu.SemaphoreType.DMA,
            pltpu.SemaphoreType.DMA((-(-n_t // TILE),)),
        ],
        compiler_params=pltpu.CompilerParams(vmem_limit_bytes=24 * 2**20),
    )(p, q_high, q_low, t)


def solution(mesh):
    n_row, n_col = mesh.shape["row"], mesh.shape["col"]

    def per_device(panel, trailing):
        a, t = pltpu.with_memory_space_constraint(panel.T, pltpu.HBM), trailing.T
        p, q_high, q_low = reduce_call(a, t, n_row, n_col)
        projections, remainder = update_call(p, q_high, q_low, t)
        return projections, remainder.T

    return jax.shard_map(
        per_device,
        mesh=mesh,
        in_specs=(P("row", "col"), P("row", "col")),
        out_specs=(P("col", None), P("row", "col")),
        check_vma=False,
    )
```
